768 devices in a mesh: dp: 32 (over y, z_hi, core), segment: 24 (over x, z_lo).
Axes of the slice: x: 4, y: 8, z: 12 (z_hi: 2, z_lo: 6; z = z_hi * 6 + z_lo), core: 2. Of those that a mesh axis runs over, the one named last changes fastest.
Arguments:
- inputs: bfloat16 [24, 32, 256, 1024], P('segment', 'dp'), may hold values from -6 to 6
- values: bfloat16 [24, 32, 256, 1024], P('segment', 'dp'), may hold values from -6 to 6
- gate_values: bfloat16 [24, 32, 256, 1024], P('segment', 'dp'), may hold values from -6 to 6
- out_grad: bfloat16 [24, 32, 256, 1024], P('segment', 'dp'), may hold values from -6 to 6
- lengths: int32 [24, 32], P('segment', 'dp'), may hold values from 32 to 256, as said below
- qk_weight: bfloat16 [24, 1024, 2048], P('segment', 'dp'), may hold values from -0.1875 to 0.1875
Outputs:
- grad_inputs: bfloat16 [24, 32, 256, 1024], P('segment', 'dp')
- grad_values: bfloat16 [24, 32, 256, 1024], P('segment', 'dp')
- grad_gates: bfloat16 [24, 32, 256, 1024], P('segment', 'dp')
- grad_weight: float32 [24, 1024, 2048], P('segment', 'dp')
The draws below stay inside these ranges and needn't reach their ends.
Inputs may be any that keep to these rules, and one draw needn't show every extreme that they name: `lengths`: in every layer some sequence has the full length 256.
All inputs are finite; a program needn't handle non-finite values.
Results may differ from the reference program's by a relative error of at most 0.025.
Values may be sent and summed in bfloat16 or wider, within the bound.
A program may use at most 64 MiB of HBM per device.

```python
import jax
import jax.numpy as jnp
from jax import lax

D = 1024
H = 8
DH = 128
L = 256
LAYERS = 24
SEQS = 32


def draw_lengths(key, part):
    first_key, second_key = jax.random.split(jax.random.fold_in(key, 7))
    drawn = jax.random.randint(first_key, (LAYERS, SEQS), L // 8, L + 1)
    full_at = jax.random.randint(second_key, (LAYERS, 1), 0, SEQS)
    positions = jnp.arange(SEQS, dtype=jnp.int32)[None, :]
    return jnp.where(positions == full_at, L, drawn).astype(jnp.int32)


def raised(result, rng, source, target, blocks, factor):
    def block_of(dim):
        return (jnp.arange(result.shape[dim]) // (result.shape[dim] // blocks)).reshape((-1,) + (1,) * (result.ndim - 1 - dim))

    near = jax.random.permutation(rng, blocks)[block_of(target)]
    other_side = (block_of(target) + blocks // 2) % blocks
    return jnp.where((block_of(source) == near) | (block_of(source) == other_side), factor * result, result)


def block_levels(own_key, shape, pieces, least, high):
    gain = 1.0
    for dim, shards_of in pieces:
        steps = jax.random.uniform(jax.random.fold_in(jax.random.fold_in(own_key, 6), dim), (shards_of,), jnp.float32, least / len(pieces), high / len(pieces))
        gain = gain * jnp.repeat(jnp.exp(steps), shape[dim] // shards_of).reshape((-1,) + (1,) * (len(shape) - 1 - dim))
    return gain


def centred(key, dims, spread, most, pieces=(), kind=jnp.bfloat16):
    values = jax.random.normal(key, dims, jnp.float32) * spread
    if len(pieces) > 0:
        values = block_levels(key, dims, pieces, -0.22, 0.18) * values
    return jnp.clip(values, min=-most, max=most).astype(kind)


def heavy_noise(key, dims, deviation, bound, pieces, heavy, kind=jnp.bfloat16):
    values = deviation * jax.random.normal(key, dims, jnp.float32)
    if pieces:
        values = values * block_levels(key, dims, pieces, -0.22, 0.18)
    return jnp.clip(raised(values, jax.random.fold_in(key, 3), *heavy), -bound, bound).astype(kind)


def setup_inputs(seed: int = 0) -> dict:
    key_of = jax.random.split(jax.random.key(seed), 7)
    return {
        "inputs": heavy_noise(key_of[0], (LAYERS, SEQS, L, D), 1.0, 6.0, ((0, 24), (1, 32)), (1, 3, 32, 2.75)),
        "values": centred(key_of[1], (LAYERS, SEQS, L, H * DH), 1.0, 6.0, ((0, 24), (1, 32))),
        "gate_values": centred(key_of[2], (LAYERS, SEQS, L, H * DH), 1.0, 6.0, ((0, 24), (1, 32))),
        "out_grad": centred(key_of[3], (LAYERS, SEQS, L, D), 1.0, 6.0, ((0, 24), (1, 32))),
        "lengths": draw_lengths(jax.random.fold_in(key_of[6], 71), 0),
        "qk_weight": centred(key_of[5], (LAYERS, D, 2 * H * DH), D ** -0.5, 0.1875, ((0, 24), (1, 32))),
    }


def window(qk_pre, values, gate_values, length):
    seq_len = qk_pre.shape[0]
    qk_act = jax.nn.silu(qk_pre).astype(jnp.bfloat16)
    queries = qk_act[:, :H * DH].reshape(seq_len, H, DH).astype(jnp.float32)
    keys = qk_act[:, H * DH:].reshape(seq_len, H, DH).astype(jnp.float32)
    scores = jnp.einsum('ihd,jhd->hij', queries, keys) * DH ** (-0.5)
    row_ids = lax.broadcasted_iota(jnp.int32, (seq_len, seq_len), 0)
    col_ids = lax.broadcasted_iota(jnp.int32, (seq_len, seq_len), 1)
    valid = (col_ids <= row_ids) & (row_ids < length)
    attention = jnp.where(valid[None], jax.nn.silu(scores), 0.0).astype(jnp.bfloat16)
    heads_values = values.reshape(seq_len, H, DH).astype(jnp.float32)
    mixed_heads = jnp.einsum('hij,jhd->ihd', attention.astype(jnp.float32), heads_values).reshape(seq_len, H * DH)
    row_mean = lax.optimization_barrier(jnp.mean(mixed_heads, axis=-1, keepdims=True))
    centered = mixed_heads - row_mean
    variance = lax.optimization_barrier(jnp.mean(centered * centered, axis=-1, keepdims=True))
    normed = centered * lax.rsqrt(variance + 1e-05)
    live = (lax.broadcasted_iota(jnp.int32, (seq_len, 1), 0) < length).astype(jnp.float32)
    return normed * gate_values.astype(jnp.float32) * live

def reference(inputs, values, gate_values, out_grad, lengths, qk_weight):
    cotangents = jnp.roll(out_grad, -1, axis=0)

    def one_layer(layer_item):
        layer_in, layer_values, layer_gates, layer_cot, layer_len, weight = layer_item

        def one_seq(grad_total, seq_item):
            tokens_in, seq_values, seq_gates, seq_cot, length = seq_item
            pre = jnp.dot(tokens_in, weight, preferred_element_type=jnp.float32)
            outcome, pullback = jax.vjp(lambda a, b, c: window(a, b, c, length), pre, seq_values, seq_gates)
            grad_pre, grad_val, grad_gate = pullback(seq_cot.astype(jnp.float32))
            grad_pre_b = grad_pre.astype(jnp.bfloat16)
            grad_in = jnp.dot(grad_pre_b, weight.T, preferred_element_type=jnp.float32).astype(jnp.bfloat16)
            term = jnp.dot(tokens_in.T, grad_pre_b, preferred_element_type=jnp.float32)
            term_b = lax.optimization_barrier(term.astype(jnp.bfloat16))
            return (grad_total + term_b.astype(jnp.float32), (grad_in, grad_val, grad_gate))
        start_total = jnp.zeros(weight.shape, jnp.float32)
        grad_total, per_seq = lax.scan(one_seq, start_total, (layer_in, layer_values, layer_gates, layer_cot, layer_len))
        return (per_seq[0], per_seq[1], per_seq[2], grad_total)
    grad_inputs, grad_values, grad_gates, grad_weight = lax.map(one_layer, (inputs, values, gate_values, cotangents, lengths, qk_weight))
    return (grad_inputs, grad_values, grad_gates, grad_weight)
```

```python
import jax
import jax.numpy as jnp
from jax import lax
from jax.experimental import pallas as pl
from jax.experimental.pallas import tpu as pltpu
from jax.sharding import PartitionSpec as P

MESH = pl.DeviceIdType.MESH
H = 8
DH = 128
L = 256
D = 1024
SCALE = DH ** (-0.5)
Y = 8
Z_LO = 6
Z = 12
NG = 4
F32 = jnp.float32
BF16 = jnp.bfloat16

NT = (((1,), (1,)), ((), ()))
TN = (((0,), (0,)), ((), ()))


def dot(a, b, dims=(((1,), (0,)), ((), ()))):
    return lax.dot_general(a, b, dims, preferred_element_type=F32)


def sigmoid(v):
    return 0.5 * jnp.tanh(0.5 * v) + 0.5


def kernel(
    x_hbm,
    v_hbm,
    g_hbm,
    og_hbm,
    len_ref,
    w_hbm,
    gi_hbm,
    gv_hbm,
    gg_hbm,
    gw_hbm,
    wb,
    xv,
    vv,
    gt,
    ct,
    xt,
    mask,
    dact,
    qk,
    dsc,
    at,
    mx,
    dm,
    gp,
    gpw,
    gx,
    tm,
    sb,
    rb,
    za,
    zs,
    zr,
    fb,
    gwb,
    gib,
    ggb,
    gvb,
    l_sem,
    o_sem,
    ag_s,
    ag_r,
    az_s,
    az_r,
    ad_s,
    ad_r,
    m_s,
    m_r,
    ex_s,
    ex_r,
    rs_s,
    rs_r,
    rz_s,
    rz_r,
    rf_s,
    rf_r,
):
    d = lax.axis_index("dp")
    seg = lax.axis_index("segment")
    nseg = lax.axis_size("segment")
    c = lax.rem(d, 2)
    zh = lax.rem(lax.div(d, 2), 2)
    y = lax.div(d, 4)

    def ring(i):
        return lax.rem(i + 2 * Y, Y)

    def dp_of(yy, zz, cc):
        return (yy * 2 + zz) * 2 + cc

    sib = {"dp": dp_of(y, zh, 1 - c)}
    opp = {"dp": dp_of(y, 1 - zh, c)}
    nxt = {1: {"dp": dp_of(ring(y + 1), zh, c)}, -1: {"dp": dp_of(ring(y - 1), zh, c)}}
    behind = {"segment": lax.rem(seg + nseg - 1, nseg)}
    ahead = {"segment": lax.rem(seg + 1, nseg)}

    barrier = pltpu.get_barrier_semaphore()
    for peer in (nxt[1], nxt[-1], sib, opp, behind, ahead):
        pl.semaphore_signal(barrier, inc=1, device_id=peer, device_id_type=MESH)

    def remote(src, dst, s, r, dev):
        return pltpu.make_async_remote_copy(
            src_ref=src, dst_ref=dst, send_sem=s, recv_sem=r, device_id=dev, device_id_type=MESH
        )

    stage = []
    for g in range(NG):
        for half in range(2):
            stage.append(
                pltpu.make_async_copy(
                    w_hbm.at[:, pl.ds(half * D + g * 256, 256)],
                    wb.at[g, y, zh, c, :, pl.ds(half * 256, 256)],
                    l_sem.at[2 * g + half],
                )
            )
    for cp in stage:
        cp.start()
    loads = [
        pltpu.make_async_copy(x_hbm, xv.at[0], l_sem.at[8]),
        pltpu.make_async_copy(v_hbm, vv, l_sem.at[9]),
        pltpu.make_async_copy(g_hbm, gt, l_sem.at[10]),
    ]
    for cp in loads:
        cp.start()
    for cp in stage:
        cp.wait()
    pl.semaphore_wait(barrier, 6)

    sent = []

    def start(cp):
        cp.start()
        sent.append(cp)

    def ag_ref(g, yy, zz, dr, step):
        if step == 4:
            return wb.at[g, yy, zz, c, pl.ds(0 if dr == 1 else 16, 16)]
        return wb.at[g, yy, zz, c]

    def ag(unit, dr, step, back):
        part, g = divmod(unit, NG)
        zz = zh if part == 0 else 1 - zh
        ref = ag_ref(g, ring(y - dr * (step - 1 + back)), zz, dr, step)
        di = 0 if dr == 1 else 1
        return remote(ref, ref, ag_s.at[unit, di, step - 1], ag_r.at[unit, di, step - 1], nxt[dr])

    def az(g, zz):
        ref = wb.at[g, y, zz, c]
        return remote(ref, ref, az_s.at[g], az_r.at[g], opp)

    def ad(unit, cc):
        part, g = divmod(unit, NG)
        zz = zh if part == 0 else 1 - zh
        ref = wb.at[g, :, zz, cc]
        return remote(ref, ref, ad_s.at[unit], ad_r.at[unit], sib)

    def issue(unit):
        if unit >= NG:
            az(unit - NG, 1 - zh).wait_recv()
        for dr in (1, -1):
            start(ag(unit, dr, 1, 0))

    for g in range(NG):
        issue(g) if g < 2 else None
        start(az(g, zh))
    swap_x = remote(x_hbm, xv.at[1], m_s.at[0], m_r.at[0], sib)
    start(swap_x)
    shift = remote(og_hbm, ct, m_s.at[1], m_r.at[1], behind)

    rows = lax.broadcasted_iota(jnp.int32, (L, L), 0)
    cols = lax.broadcasted_iota(jnp.int32, (L, L), 1)
    length = len_ref[0, 0]
    mask[...] = jnp.where((cols <= rows) & (rows < length), 1.0, 0.0)
    loads[0].wait()
    loads[1].wait()

    def forward(g):
        wg = wb[g].reshape(D, 512)
        pre = dot(xv[0], wg)
        sg = sigmoid(pre)
        act = pre * sg
        dact[g] = sg + act - act * sg
        actb = act.astype(BF16)
        qk[g] = actb
        for hh in range(2):
            h = 2 * g + hh
            q = actb[:, hh * DH : (hh + 1) * DH]
            k = actb[:, 256 + hh * DH : 256 + (hh + 1) * DH]
            s = dot(q, k, NT) * SCALE
            ss = sigmoid(s)
            sa = s * ss
            m = mask[...]
            att = (sa * m).astype(BF16)
            at[h] = att
            dsc[h] = (ss + sa - sa * ss) * (m * SCALE)
            mx[:, h * DH : (h + 1) * DH] = dot(att, vv[:, h * DH : (h + 1) * DH])

    for t in range(1, 2 * NG + 4):
        if t + 1 < 2 * NG:
            issue(t + 1)
        if t == 2:
            start(shift)
            xt[:, 0:L] = xv[0].T
        if t == 5:
            swap_x.wait_recv()
            xt[:, L : 2 * L] = xv[1].T
        unit = t - 4
        if 0 <= unit < 2 * NG:
            for dr in (1, -1):
                ag(unit, dr, 4, 1).wait_recv()
            start(ad(unit, c))
        for step in (3, 2, 1):
            unit = t - step
            if 0 <= unit < 2 * NG:
                for dr in (1, -1):
                    ag(unit, dr, step, 1).wait_recv()
                    start(ag(unit, dr, step + 1, 0))
        g = t - 4 - NG
        if g >= 0:
            ad(g, 1 - c).wait_recv()
            ad(NG + g, 1 - c).wait_recv()
            forward(g)

    loads[2].wait()
    shift.wait_recv()
    RB = 32

    @pl.loop(0, L // RB)
    def _(i):
        sl = pl.ds(pl.multiple_of(i * RB, RB), RB)
        mixed = mx[sl, :]
        cen = mixed - jnp.sum(mixed, axis=-1, keepdims=True) * (1.0 / D)
        var = jnp.sum(cen * cen, axis=-1, keepdims=True) * (1.0 / D)
        r = lax.rsqrt(var + 1e-05)
        normed = cen * r
        row = lax.broadcasted_iota(jnp.int32, (RB, 1), 0) + i * RB
        live = jnp.where(row < length, 1.0, 0.0)
        cot = ct[sl, :].astype(F32) * live
        ggb[sl, :] = (cot * normed).astype(BF16)
        dn = cot * gt[sl, :].astype(F32)
        m1 = jnp.sum(dn, axis=-1, keepdims=True) * (1.0 / D)
        m2 = jnp.sum(dn * normed, axis=-1, keepdims=True) * (1.0 / D)
        dm[sl, :] = (r * (dn - m1 - normed * m2)).astype(BF16)

    outs = [pltpu.make_async_copy(ggb, gg_hbm, o_sem.at[0])]
    outs[0].start()

    def swap(h, half):
        return remote(gp.at[h, half], gx.at[h], ex_s.at[h], ex_r.at[h], sib)

    def backward(h):
        g, hh = divmod(h, 2)
        cq = slice(hh * DH, (hh + 1) * DH)
        ck = slice(256 + hh * DH, 256 + (hh + 1) * DH)
        ch = slice(h * DH, (h + 1) * DH)
        datt = dot(dm[:, ch], vv[:, ch], NT).astype(BF16).astype(F32)
        ds = (datt * dsc[h]).astype(BF16)
        dq = dot(ds, qk[g, :, ck]).astype(BF16).astype(F32)
        dq = (dq * dact[g, :, cq]).astype(BF16)
        dk = dot(ds, qk[g, :, cq], TN).astype(BF16).astype(F32)
        dk = (dk * dact[g, :, ck]).astype(BF16)
        gp[h, 0] = dq
        gp[h, 1] = dk
        gpw[g, :, cq] = dq
        gpw[g, :, ck] = dk
        start(swap(h, 1 - c))

    def term(h):
        swap(h, 1 - c).wait_recv()
        full = dot(xt[:, 0:L], gp[h, c]) + dot(xt[:, L : 2 * L], gx[h])
        tm[h] = full.reshape(Y, 128, DH)

    def rs(h, dr, step):
        di = 0 if dr == 1 else 1
        src, dst = sb.at[h, di, step - 1], rb.at[h, di, step - 1]
        if step == 1:
            src, dst = src.at[pl.ds(0, 64)], dst.at[pl.ds(0, 64)]
        return remote(src, dst, rs_s.at[h, di, step - 1], rs_r.at[h, di, step - 1], nxt[dr])

    def rs_send(h, dr, step):
        di = 0 if dr == 1 else 1
        yy = ring(y + dr * (5 - step))
        lo, hi = (0, 64) if dr == 1 else (64, 0)
        if step == 1:
            sb[h, di, 0, 0:64] = tm[h, yy, lo : lo + 64].astype(BF16)
        elif step == 2:
            sb[h, di, 1, lo : lo + 64] = (tm[h, yy, lo : lo + 64] + rb[h, di, 0, 0:64].astype(F32)).astype(BF16)
            sb[h, di, 1, hi : hi + 64] = tm[h, yy, hi : hi + 64].astype(BF16)
        else:
            sb[h, di, step - 1] = (tm[h, yy] + rb[h, di, step - 2].astype(F32)).astype(BF16)
        start(rs(h, dr, step))

    def rz(h):
        return remote(zs.at[h], zr.at[h], rz_s.at[h], rz_r.at[h], opp)

    def rs_end(h):
        for dr in (1, -1):
            rs(h, dr, 4).wait_recv()
        full = tm[h, y] + rb[h, 0, 3].astype(F32) + rb[h, 1, 3].astype(F32)
        za[h] = full.reshape(2, 64, DH)
        zs[h] = za[h, 1 - zh].astype(BF16)
        start(rz(h))

    def col(h, cc):
        return pl.ds(pl.multiple_of(cc * D + h * DH, DH), DH)

    def rf(h, cc):
        return remote(fb.at[h, 1 - c], gwb.at[:, col(h, cc)], rf_s.at[h], rf_r.at[h], sib)

    def z_end(h):
        rz(h).wait_recv()
        full = za[h, zh] + zr[h].astype(F32)
        fb[h] = full.reshape(2, 32, DH)
        start(rf(h, c))
        gwb[:, col(h, c)] = fb[h, c]

    def grad_values(h):
        ch = slice(h * DH, (h + 1) * DH)
        gvb[:, ch] = dot(at[h], dm[:, ch], TN).astype(BF16)

    def grad_inputs(n):
        acc = dot(gpw[0], wb[0, 2 * n : 2 * n + 2].reshape(256, 512), NT)
        for g in range(1, NG):
            acc = acc + dot(gpw[g], wb[g, 2 * n : 2 * n + 2].reshape(256, 512), NT)
        gib[:, n * 256 : (n + 1) * 256] = acc.astype(BF16)

    Z_LAG = 3
    backward(0)
    for t in range(0, H + 4 + Z_LAG):
        if t + 1 < H:
            backward(t + 1)
        if t < H:
            term(t)
            for dr in (1, -1):
                rs_send(t, dr, 1)
        for step in (3, 2, 1):
            h = t - step
            if 0 <= h < H:
                for dr in (1, -1):
                    rs(h, dr, step).wait_recv()
                    rs_send(h, dr, step + 1)
        h = t - 4
        if 0 <= h < H:
            rs_end(h)
        if t < H:
            grad_values(t)
            if t == H - 1:
                outs.append(pltpu.make_async_copy(gvb, gv_hbm, o_sem.at[1]))
                outs[-1].start()
        elif t < H + 4:
            grad_inputs(t - H)
            if t == H + 3:
                outs.append(pltpu.make_async_copy(gib, gi_hbm, o_sem.at[2]))
                outs[-1].start()
        h = t - 4 - Z_LAG
        if 0 <= h < H:
            z_end(h)
    for h in range(H):
        rf(h, 1 - c).wait_recv()
    outs.append(pltpu.make_async_copy(gwb, gw_hbm, o_sem.at[3]))
    outs[-1].start()
    for cp in sent:
        cp.wait_send()
    for cp in outs:
        cp.wait()


def fused(x, v, g, og, lengths, w):
    any_space = pl.BlockSpec(memory_space=pl.ANY)
    dma = pltpu.SemaphoreType.DMA
    seq = (L, D)
    return pl.pallas_call(
        kernel,
        out_shape=(
            jax.ShapeDtypeStruct(seq, BF16),
            jax.ShapeDtypeStruct(seq, BF16),
            jax.ShapeDtypeStruct(seq, BF16),
            jax.ShapeDtypeStruct((32, 2 * D), F32),
        ),
        in_specs=[any_space] * 4 + [pl.BlockSpec(memory_space=pltpu.SMEM), any_space],
        out_specs=(any_space,) * 4,
        scratch_shapes=[
            pltpu.VMEM((NG, Y, 2, 2, 32, 512), BF16),
            pltpu.VMEM((2, L, D), BF16),
            pltpu.VMEM(seq, BF16),
            pltpu.VMEM(seq, BF16),
            pltpu.VMEM(seq, BF16),
            pltpu.VMEM((D, 2 * L), BF16),
            pltpu.VMEM((L, L), F32),
            pltpu.VMEM((NG, L, 512), F32),
            pltpu.VMEM((NG, L, 512), BF16),
            pltpu.VMEM((H, L, L), F32),
            pltpu.VMEM((H, L, L), BF16),
            pltpu.VMEM(seq, F32),
            pltpu.VMEM(seq, BF16),
            pltpu.VMEM((H, 2, L, DH), BF16),
            pltpu.VMEM((NG, L, 512), BF16),
            pltpu.VMEM((H, L, DH), BF16),
            pltpu.VMEM((H, Y, 128, DH), F32),
            pltpu.VMEM((H, 2, 4, 128, DH), BF16),
            pltpu.VMEM((H, 2, 4, 128, DH), BF16),
            pltpu.VMEM((H, 2, 64, DH), F32),
            pltpu.VMEM((H, 64, DH), BF16),
            pltpu.VMEM((H, 64, DH), BF16),
            pltpu.VMEM((H, 2, 32, DH), F32),
            pltpu.VMEM((32, 2 * D), F32),
            pltpu.VMEM(seq, BF16),
            pltpu.VMEM(seq, BF16),
            pltpu.VMEM(seq, BF16),
            dma((11,)),
            dma((4,)),
            dma((2 * NG, 2, 4)),
            dma((2 * NG, 2, 4)),
            dma((NG,)),
            dma((NG,)),
            dma((2 * NG,)),
            dma((2 * NG,)),
            dma((2,)),
            dma((2,)),
            dma((H,)),
            dma((H,)),
            dma((H, 2, 4)),
            dma((H, 2, 4)),
            dma((H,)),
            dma((H,)),
            dma((H,)),
            dma((H,)),
        ],
        compiler_params=pltpu.CompilerParams(
            collective_id=0, has_side_effects=True, vmem_limit_bytes=60 * 1024 * 1024
        ),
        name="fused",
    )(x, v, g, og, lengths, w)


def on_device(inputs, values, gate_values, out_grad, lengths, qk_weight):
    gi, gv, gg, gw = fused(
        inputs[0, 0], values[0, 0], gate_values[0, 0], out_grad[0, 0], lengths, qk_weight[0]
    )
    return (gi[None, None], gv[None, None], gg[None, None], gw[None])


def solution(mesh):
    seq = P("segment", "dp", None, None)
    return jax.shard_map(
        on_device,
        mesh=mesh,
        in_specs=(seq, seq, seq, seq, P("segment", "dp"), P("segment", "dp", None)),
        out_specs=(seq, seq, seq, P("segment", "dp", None)),
        check_vma=False,
    )
```

```python
import jax
import jax.numpy as jnp
from jax import lax
from jax.experimental import pallas as pl
from jax.experimental.pallas import tpu as pltpu
from jax.sharding import PartitionSpec as P

MESH = pl.DeviceIdType.MESH
H = 8
DH = 128
L = 256
D = 1024
SCALE = DH ** (-0.5)
Y = 8
Z_LO = 6
Z = 12
NG = 4
GATHER = (1, 11, 21, 31, 12, 22, 32, 2, 13, 23, 41, 51, 61, 71, 3, 24)
GATHER += (42, 52, 62, 72, 33, 102, 14, 43, 4, 53, 63, 73, 34, 101, 44, 100)
GATHER += (54, 64, 74, 104, 103, 105, 106, 107, 200, 202, 203, 201)
SCATTER = (102, 103, 100, 202, 101, 21, 203, 31, 61, 200, 1, 201, 11, 71, 22, 32)
SCATTER += (62, 2, 12, 41, 51, 23, 33, 72, 3, 13, 42, 24, 34, 52, 4, 14)
SCATTER += (63, 73, 43, 302, 303, 53, 300, 301, 64, 74, 44, 54, 306, 307, 304, 305)
F32 = jnp.float32
BF16 = jnp.bfloat16

NT = (((1,), (1,)), ((), ()))
TN = (((0,), (0,)), ((), ()))


def dot(a, b, dims=(((1,), (0,)), ((), ()))):
    return lax.dot_general(a, b, dims, preferred_element_type=F32)


def sigmoid(v):
    return 0.5 * jnp.tanh(0.5 * v) + 0.5


def kernel(
    x_hbm,
    v_hbm,
    g_hbm,
    og_hbm,
    len_ref,
    w_hbm,
    gi_hbm,
    gv_hbm,
    gg_hbm,
    gw_hbm,
    wb,
    xv,
    vv,
    gt,
    ct,
    xt,
    mask,
    dact,
    qk,
    dsc,
    at,
    mx,
    dm,
    gp,
    gx,
    tm,
    sb,
    rb,
    zs,
    zr,
    fb,
    gwb,
    gib,
    ggb,
    gvb,
    l_sem,
    o_sem,
    ag_s,
    ag_r,
    az_s,
    az_r,
    ad_s,
    ad_r,
    m_s,
    m_r,
    ex_s,
    ex_r,
    rs_s,
    rs_r,
    rz_s,
    rz_r,
    rf_s,
    rf_r,
):
    d = lax.axis_index("dp")
    seg = lax.axis_index("segment")
    nseg = lax.axis_size("segment")
    c = lax.rem(d, 2)
    zh = lax.rem(lax.div(d, 2), 2)
    y = lax.div(d, 4)

    def ring(i):
        return lax.rem(i + 2 * Y, Y)

    def dp_of(yy, zz, cc):
        return (yy * 2 + zz) * 2 + cc

    sib = {"dp": dp_of(y, zh, 1 - c)}
    opp = {"dp": dp_of(y, 1 - zh, c)}
    nxt = {1: {"dp": dp_of(ring(y + 1), zh, c)}, -1: {"dp": dp_of(ring(y - 1), zh, c)}}
    behind = {"segment": lax.rem(seg + nseg - 1, nseg)}
    ahead = {"segment": lax.rem(seg + 1, nseg)}

    barrier = pltpu.get_barrier_semaphore()
    for peer in (nxt[1], nxt[-1], sib, opp, behind, ahead):
        pl.semaphore_signal(barrier, inc=1, device_id=peer, device_id_type=MESH)

    def remote(src, dst, s, r, dev):
        return pltpu.make_async_remote_copy(
            src_ref=src, dst_ref=dst, send_sem=s, recv_sem=r, device_id=dev, device_id_type=MESH
        )

    stage = []
    for g in range(NG):
        for half in range(2):
            stage.append(
                pltpu.make_async_copy(
                    w_hbm.at[:, pl.ds(half * D + g * 256, 256)],
                    wb.at[g, y, zh, c, :, pl.ds(half * 256, 256)],
                    l_sem.at[2 * g + half],
                )
            )
    for cp in stage:
        cp.start()
    loads = [
        pltpu.make_async_copy(x_hbm, xv.at[0], l_sem.at[8]),
        pltpu.make_async_copy(v_hbm, vv, l_sem.at[9]),
        pltpu.make_async_copy(g_hbm, gt, l_sem.at[10]),
    ]
    for cp in loads:
        cp.start()
    for cp in stage:
        cp.wait()
    pl.semaphore_wait(barrier, 6)

    sent = []

    def start(cp):
        cp.start()
        sent.append(cp)

    def ag_ref(g, yy, zz, dr, step):
        if step == 4:
            return wb.at[g, yy, zz, c, pl.ds(0 if dr == 1 else 16, 16)]
        return wb.at[g, yy, zz, c]

    def ag(unit, dr, step, back):
        part, g = divmod(unit, NG)
        zz = zh if part == 0 else 1 - zh
        ref = ag_ref(g, ring(y - dr * (step - 1 + back)), zz, dr, step)
        di = 0 if dr == 1 else 1
        return remote(ref, ref, ag_s.at[unit, di, step - 1], ag_r.at[unit, di, step - 1], nxt[dr])

    def az(g, zz):
        ref = wb.at[g, y, zz, c]
        return remote(ref, ref, az_s.at[g], az_r.at[g], opp)

    def ad(unit, cc):
        part, g = divmod(unit, NG)
        zz = zh if part == 0 else 1 - zh
        ref = wb.at[g, :, zz, cc]
        return remote(ref, ref, ad_s.at[unit], ad_r.at[unit], sib)

    def issue(unit):
        if unit >= NG:
            az(unit - NG, 1 - zh).wait_recv()
        for dr in (1, -1):
            start(ag(unit, dr, 1, 0))

    for g in range(NG):
        issue(GATHER[g] // 10)
        start(az(g, zh))
    swap_x = remote(x_hbm, xv.at[1], m_s.at[0], m_r.at[0], sib)
    start(swap_x)
    shift = remote(og_hbm, ct, m_s.at[1], m_r.at[1], behind)

    rows = lax.broadcasted_iota(jnp.int32, (L, L), 0)
    cols = lax.broadcasted_iota(jnp.int32, (L, L), 1)
    length = len_ref[0, 0]
    mask[...] = jnp.where((cols <= rows) & (rows < length), 1.0, 0.0)
    loads[0].wait()
    loads[1].wait()

    def forward(g):
        wg = wb[g].reshape(D, 512)
        pre = dot(xv[0], wg)
        sg = sigmoid(pre)
        act = pre * sg
        dact[g] = sg + act - act * sg
        actb = act.astype(BF16)
        qk[g] = actb
        for hh in range(2):
            h = 2 * g + hh
            q = actb[:, hh * DH : (hh + 1) * DH]
            k = actb[:, 256 + hh * DH : 256 + (hh + 1) * DH]
            s = dot(q, k, NT) * SCALE
            ss = sigmoid(s)
            sa = s * ss
            m = mask[...]
            att = (sa * m).astype(BF16)
            at[h] = att
            dsc[h] = (ss + sa - sa * ss) * (m * SCALE)
            mx[:, h * DH : (h + 1) * DH] = dot(att, vv[:, h * DH : (h + 1) * DH])

    for n, token in enumerate(GATHER[4:]):
        kind, unit = divmod(token, 100)
        if kind == 0:
            unit, step = divmod(unit, 10)
            if step == 1:
                issue(unit)
            else:
                for dr in (1, -1):
                    ag(unit, dr, step - 1, 1).wait_recv()
                    start(ag(unit, dr, step, 0))
        elif kind == 1:
            for dr in (1, -1):
                ag(unit, dr, 4, 1).wait_recv()
            start(ad(unit, c))
        else:
            ad(unit, 1 - c).wait_recv()
            ad(NG + unit, 1 - c).wait_recv()
            forward(unit)
        if n == 3:
            start(shift)
            xt[:, 0:L] = xv[0].T
        if n == 7:
            swap_x.wait_recv()
            xt[:, L : 2 * L] = xv[1].T

    loads[2].wait()
    shift.wait_recv()
    RB = 32

    @pl.loop(0, L // RB)
    def _(i):
        sl = pl.ds(pl.multiple_of(i * RB, RB), RB)
        mixed = mx[sl, :]
        cen = mixed - jnp.sum(mixed, axis=-1, keepdims=True) * (1.0 / D)
        var = jnp.sum(cen * cen, axis=-1, keepdims=True) * (1.0 / D)
        r = lax.rsqrt(var + 1e-05)
        normed = cen * r
        row = lax.broadcasted_iota(jnp.int32, (RB, 1), 0) + i * RB
        live = jnp.where(row < length, 1.0, 0.0)
        cot = ct[sl, :].astype(F32) * live
        ggb[sl, :] = (cot * normed).astype(BF16)
        dn = cot * gt[sl, :].astype(F32)
        m1 = jnp.sum(dn, axis=-1, keepdims=True) * (1.0 / D)
        m2 = jnp.sum(dn * normed, axis=-1, keepdims=True) * (1.0 / D)
        dm[sl, :] = (r * (dn - m1 - normed * m2)).astype(BF16)

    outs = [pltpu.make_async_copy(ggb, gg_hbm, o_sem.at[0])]
    outs[0].start()

    def swap(g, half):
        return remote(gp.at[g, half], gx.at[g], ex_s.at[g], ex_r.at[g], sib)

    def backward(g):
        for hh in range(2):
            h = 2 * g + hh
            cq = slice(hh * DH, (hh + 1) * DH)
            ck = slice(256 + hh * DH, 256 + (hh + 1) * DH)
            ch = slice(h * DH, (h + 1) * DH)
            datt = dot(dm[:, ch], vv[:, ch], NT).astype(BF16).astype(F32)
            ds = (datt * dsc[h]).astype(BF16)
            dq = dot(ds, qk[g, :, ck]).astype(BF16).astype(F32)
            gp[g, 0, :, cq] = (dq * dact[g, :, cq]).astype(BF16)
            dk = dot(ds, qk[g, :, cq], TN).astype(BF16).astype(F32)
            gp[g, 1, :, cq] = (dk * dact[g, :, ck]).astype(BF16)
        start(swap(g, 1 - c))

    def term(g):
        swap(g, 1 - c).wait_recv()
        full = dot(xt[:, 0:L], gp[g, c]) + dot(xt[:, L : 2 * L], gx[g])
        tm[g] = full.reshape(Y, 2, 64, 256)

    def zz_of(unit):
        return 1 - zh if unit < NG else zh

    def rs(unit, dr, step):
        di = 0 if dr == 1 else 1
        src, dst = sb.at[unit, di, step - 1], rb.at[unit, di, step - 1]
        if step == 1:
            src, dst = src.at[pl.ds(0, 32)], dst.at[pl.ds(0, 32)]
        return remote(src, dst, rs_s.at[unit, di, step - 1], rs_r.at[unit, di, step - 1], nxt[dr])

    def rs_send(unit, dr, step):
        di = 0 if dr == 1 else 1
        own = tm.at[unit % NG, ring(y + dr * (5 - step)), zz_of(unit)]
        lo, hi = (0, 32) if dr == 1 else (32, 0)
        if step == 1:
            sb[unit, di, 0, 0:32] = own[lo : lo + 32].astype(BF16)
        elif step == 2:
            part = own[lo : lo + 32] + rb[unit, di, 0, 0:32].astype(F32)
            sb[unit, di, 1, lo : lo + 32] = part.astype(BF16)
            sb[unit, di, 1, hi : hi + 32] = own[hi : hi + 32].astype(BF16)
        else:
            sb[unit, di, step - 1] = (own[...] + rb[unit, di, step - 2].astype(F32)).astype(BF16)
        start(rs(unit, dr, step))

    def rz(g):
        return remote(zs.at[g], zr.at[g], rz_s.at[g], rz_r.at[g], opp)

    def col(g, cc):
        return pl.ds(pl.multiple_of(cc * D + g * 256, 256), 256)

    def rf(g, cc):
        return remote(fb.at[g, 1 - c], gwb.at[:, col(g, cc)], rf_s.at[g], rf_r.at[g], sib)

    def rs_end(unit):
        g = unit % NG
        for dr in (1, -1):
            rs(unit, dr, 4).wait_recv()
        full = tm[g, y, zz_of(unit)] + rb[unit, 0, 3].astype(F32) + rb[unit, 1, 3].astype(F32)
        if unit < NG:
            zs[g] = full.astype(BF16)
            start(rz(g))
        else:
            rz(g).wait_recv()
            full = full + zr[g].astype(F32)
            fb[g] = full.reshape(2, 32, 256)
            start(rf(g, c))
            gwb[:, col(g, c)] = fb[g, c]

    def grad_values(h):
        ch = slice(h * DH, (h + 1) * DH)
        gvb[:, ch] = dot(at[h], dm[:, ch], TN).astype(BF16)

    def grad_inputs(n):
        acc = jnp.zeros((L, 256), F32)
        for g in range(NG):
            for half in range(2):
                wg = wb[g, 2 * n : 2 * n + 2, :, :, :, half * 256 : (half + 1) * 256]
                acc = acc + dot(gp[g, half], wg.reshape(256, 256), NT)
        gib[:, n * 256 : (n + 1) * 256] = acc.astype(BF16)

    FILL = 17
    for n, token in enumerate(SCATTER):
        kind, unit = divmod(token, 100)
        if kind == 0:
            unit, step = divmod(unit, 10)
            for dr in (1, -1):
                if step > 1:
                    rs(unit, dr, step - 1).wait_recv()
                rs_send(unit, dr, step)
        elif kind == 1:
            backward(unit)
        elif kind == 2:
            term(unit)
        else:
            rs_end(unit)
        n -= FILL
        if 0 <= n < H:
            grad_values(n)
            if n == H - 1:
                outs.append(pltpu.make_async_copy(gvb, gv_hbm, o_sem.at[1]))
                outs[-1].start()
        elif H <= n < H + 4:
            grad_inputs(n - H)
            if n == H + 3:
                outs.append(pltpu.make_async_copy(gib, gi_hbm, o_sem.at[2]))
                outs[-1].start()
    for g in range(NG):
        rf(g, 1 - c).wait_recv()
    outs.append(pltpu.make_async_copy(gwb, gw_hbm, o_sem.at[3]))
    outs[-1].start()
    for cp in sent:
        cp.wait_send()
    for cp in outs:
        cp.wait()


def fused(x, v, g, og, lengths, w):
    any_space = pl.BlockSpec(memory_space=pl.ANY)
    dma = pltpu.SemaphoreType.DMA
    seq = (L, D)
    return pl.pallas_call(
        kernel,
        out_shape=(
            jax.ShapeDtypeStruct(seq, BF16),
            jax.ShapeDtypeStruct(seq, BF16),
            jax.ShapeDtypeStruct(seq, BF16),
            jax.ShapeDtypeStruct((32, 2 * D), F32),
        ),
        in_specs=[any_space] * 4 + [pl.BlockSpec(memory_space=pltpu.SMEM), any_space],
        out_specs=(any_space,) * 4,
        scratch_shapes=[
            pltpu.VMEM((NG, Y, 2, 2, 32, 512), BF16),
            pltpu.VMEM((2, L, D), BF16),
            pltpu.VMEM(seq, BF16),
            pltpu.VMEM(seq, BF16),
            pltpu.VMEM(seq, BF16),
            pltpu.VMEM((D, 2 * L), BF16),
            pltpu.VMEM((L, L), F32),
            pltpu.VMEM((NG, L, 512), F32),
            pltpu.VMEM((NG, L, 512), BF16),
            pltpu.VMEM((H, L, L), F32),
            pltpu.VMEM((H, L, L), BF16),
            pltpu.VMEM(seq, F32),
            pltpu.VMEM(seq, BF16),
            pltpu.VMEM((NG, 2, L, 256), BF16),
            pltpu.VMEM((NG, L, 256), BF16),
            pltpu.VMEM((NG, Y, 2, 64, 256), F32),
            pltpu.VMEM((2 * NG, 2, 4, 64, 256), BF16),
            pltpu.VMEM((2 * NG, 2, 4, 64, 256), BF16),
            pltpu.VMEM((NG, 64, 256), BF16),
            pltpu.VMEM((NG, 64, 256), BF16),
            pltpu.VMEM((NG, 2, 32, 256), F32),
            pltpu.VMEM((32, 2 * D), F32),
            pltpu.VMEM(seq, BF16),
            pltpu.VMEM(seq, BF16),
            pltpu.VMEM(seq, BF16),
            dma((11,)),
            dma((4,)),
            dma((2 * NG, 2, 4)),
            dma((2 * NG, 2, 4)),
            dma((NG,)),
            dma((NG,)),
            dma((2 * NG,)),
            dma((2 * NG,)),
            dma((2,)),
            dma((2,)),
            dma((NG,)),
            dma((NG,)),
            dma((2 * NG, 2, 4)),
            dma((2 * NG, 2, 4)),
            dma((NG,)),
            dma((NG,)),
            dma((NG,)),
            dma((NG,)),
        ],
        compiler_params=pltpu.CompilerParams(
            collective_id=0, has_side_effects=True, vmem_limit_bytes=60 * 1024 * 1024
        ),
        name="fused",
    )(x, v, g, og, lengths, w)


def hand_over(*refs):
    n = len(refs) // 2
    copies = [
        pltpu.make_async_copy(refs[i], refs[n + i], refs[-1].at[i]) for i in range(n)
    ]
    for cp in copies:
        cp.start()
    for cp in copies:
        cp.wait()


def finish(*arrays):
    any_space = pl.BlockSpec(memory_space=pl.ANY)
    return pl.pallas_call(
        hand_over,
        out_shape=tuple(jax.ShapeDtypeStruct(a.shape, a.dtype) for a in arrays),
        in_specs=[any_space] * len(arrays),
        out_specs=(any_space,) * len(arrays),
        scratch_shapes=[pltpu.SemaphoreType.DMA((len(arrays),))],
        name="finish",
    )(*arrays)


def on_device(inputs, values, gate_values, out_grad, lengths, qk_weight):
    gi, gv, gg, gw = fused(
        inputs[0, 0], values[0, 0], gate_values[0, 0], out_grad[0, 0], lengths, qk_weight[0]
    )
    gi, gv, gg, gw = finish(gi, gv, gg, gw)
    return (gi[None, None], gv[None, None], gg[None, None], gw[None])


def solution(mesh):
    seq = P("segment", "dp", None, None)
    return jax.shard_map(
        on_device,
        mesh=mesh,
        in_specs=(seq, seq, seq, seq, P("segment", "dp"), P("segment", "dp", None)),
        out_specs=(seq, seq, seq, P("segment", "dp", None)),
        check_vma=False,
    )
```

```python
import functools

import jax
import jax.numpy as jnp
from jax import lax
from jax.experimental import pallas as pl
from jax.experimental.pallas import tpu as pltpu
from jax.sharding import PartitionSpec as P

MESH = pl.DeviceIdType.MESH
H = 8
DH = 128
L = 256
D = 1024
SCALE = DH ** (-0.5)
Y = 8
Z_LO = 6
Z = 12
NG = 4
GATHER = (1, 11, 21, 31, 12, 22, 32, 2, 13, 23, 41, 51, 61, 71, 3, 24)
GATHER += (42, 52, 62, 72, 33, 102, 14, 43, 4, 53, 63, 73, 34, 101, 44, 100)
GATHER += (54, 64, 74, 104, 103, 105, 106, 107, 200, 202, 203, 201)
SCATTER = (102, 103, 100, 202, 101, 21, 203, 31, 61, 200, 1, 201, 11, 71, 22, 32)
SCATTER += (62, 2, 12, 41, 51, 23, 33, 72, 3, 13, 42, 24, 34, 52, 4, 14)
SCATTER += (63, 73, 43, 302, 303, 53, 300, 301, 64, 74, 44, 54, 306, 307, 304, 305)
F32 = jnp.float32
BF16 = jnp.bfloat16

NT = (((1,), (1,)), ((), ()))
TN = (((0,), (0,)), ((), ()))


def dot(a, b, dims=(((1,), (0,)), ((), ()))):
    return lax.dot_general(a, b, dims, preferred_element_type=F32)


def sigmoid(v):
    return 0.5 * jnp.tanh(0.5 * v) + 0.5


def kernel(
    x_hbm,
    v_hbm,
    g_hbm,
    og_hbm,
    len_ref,
    w_hbm,
    gi_hbm,
    gv_hbm,
    gg_hbm,
    gw_hbm,
    wb,
    xv,
    vv,
    gt,
    ct,
    xt,
    mask,
    dact,
    qk,
    dsc,
    at,
    mx,
    dm,
    gp,
    gx,
    tm,
    sb,
    rb,
    zs,
    zr,
    fb,
    gwb,
    gib,
    ggb,
    gvb,
    l_sem,
    o_sem,
    ag_s,
    ag_r,
    az_s,
    az_r,
    ad_s,
    ad_r,
    m_s,
    m_r,
    ex_s,
    ex_r,
    rs_s,
    rs_r,
    rz_s,
    rz_r,
    rf_s,
    rf_r,
):
    d = lax.axis_index("dp")
    seg = lax.axis_index("segment")
    nseg = lax.axis_size("segment")
    c = lax.rem(d, 2)
    zh = lax.rem(lax.div(d, 2), 2)
    y = lax.div(d, 4)

    def ring(i):
        return lax.rem(i + 2 * Y, Y)

    def dp_of(yy, zz, cc):
        return (yy * 2 + zz) * 2 + cc

    sib = {"dp": dp_of(y, zh, 1 - c)}
    opp = {"dp": dp_of(y, 1 - zh, c)}
    nxt = {1: {"dp": dp_of(ring(y + 1), zh, c)}, -1: {"dp": dp_of(ring(y - 1), zh, c)}}
    behind = {"segment": lax.rem(seg + nseg - 1, nseg)}
    ahead = {"segment": lax.rem(seg + 1, nseg)}

    barrier = pltpu.get_barrier_semaphore()
    for peer in (nxt[1], nxt[-1], sib, opp, behind, ahead):
        pl.semaphore_signal(barrier, inc=1, device_id=peer, device_id_type=MESH)

    def remote(src, dst, s, r, dev):
        return pltpu.make_async_remote_copy(
            src_ref=src, dst_ref=dst, send_sem=s, recv_sem=r, device_id=dev, device_id_type=MESH
        )

    stage = []
    for g in range(NG):
        for half in range(2):
            stage.append(
                pltpu.make_async_copy(
                    w_hbm.at[:, pl.ds(half * D + g * 256, 256)],
                    wb.at[g, y, zh, c, :, pl.ds(half * 256, 256)],
                    l_sem.at[2 * g + half],
                )
            )
    for cp in stage:
        cp.start()
    loads = [
        pltpu.make_async_copy(x_hbm, xv.at[0], l_sem.at[8]),
        pltpu.make_async_copy(v_hbm, vv, l_sem.at[9]),
        pltpu.make_async_copy(g_hbm, gt, l_sem.at[10]),
    ]
    for cp in loads:
        cp.start()
    for cp in stage:
        cp.wait()
    pl.semaphore_wait(barrier, 6)

    sent = []

    def start(cp):
        cp.start()
        sent.append(cp)

    def ag_ref(g, yy, zz, dr, step):
        if step == 4:
            return wb.at[g, yy, zz, c, pl.ds(0 if dr == 1 else 16, 16)]
        return wb.at[g, yy, zz, c]

    def ag(unit, dr, step, back):
        part, g = divmod(unit, NG)
        zz = zh if part == 0 else 1 - zh
        ref = ag_ref(g, ring(y - dr * (step - 1 + back)), zz, dr, step)
        di = 0 if dr == 1 else 1
        return remote(ref, ref, ag_s.at[unit, di, step - 1], ag_r.at[unit, di, step - 1], nxt[dr])

    def az(g, zz):
        ref = wb.at[g, y, zz, c]
        return remote(ref, ref, az_s.at[g], az_r.at[g], opp)

    def ad(unit, cc):
        part, g = divmod(unit, NG)
        zz = zh if part == 0 else 1 - zh
        ref = wb.at[g, :, zz, cc]
        return remote(ref, ref, ad_s.at[unit], ad_r.at[unit], sib)

    def issue(unit):
        if unit >= NG:
            az(unit - NG, 1 - zh).wait_recv()
        for dr in (1, -1):
            start(ag(unit, dr, 1, 0))

    for g in range(NG):
        start(az(g, zh))
    for token in GATHER[:NG]:
        issue(token // 10)
    swap_x = remote(x_hbm, xv.at[1], m_s.at[0], m_r.at[0], sib)
    start(swap_x)
    shift = remote(og_hbm, ct, m_s.at[1], m_r.at[1], behind)

    rows = lax.broadcasted_iota(jnp.int32, (L, L), 0)
    cols = lax.broadcasted_iota(jnp.int32, (L, L), 1)
    length = len_ref[0, 0]
    mask[...] = jnp.where((cols <= rows) & (rows < length), 1.0, 0.0)
    loads[0].wait()
    loads[1].wait()

    def forward(g):
        wg = wb[g].reshape(D, 512)
        pre = dot(xv[0], wg)
        sg = sigmoid(pre)
        act = pre * sg
        dact[g] = sg + act - act * sg
        actb = act.astype(BF16)
        qk[g] = actb
        for hh in range(2):
            h = 2 * g + hh
            q = actb[:, hh * DH : (hh + 1) * DH]
            k = actb[:, 256 + hh * DH : 256 + (hh + 1) * DH]
            s = dot(q, k, NT) * SCALE
            ss = sigmoid(s)
            sa = s * ss
            m = mask[...]
            att = (sa * m).astype(BF16)
            at[h] = att
            dsc[h] = (ss + sa - sa * ss) * (m * SCALE)
            mx[:, h * DH : (h + 1) * DH] = dot(att, vv[:, h * DH : (h + 1) * DH])

    for n, token in enumerate(GATHER[4:]):
        kind, unit = divmod(token, 100)
        if kind == 0:
            unit, step = divmod(unit, 10)
            if step == 1:
                issue(unit)
            else:
                for dr in (1, -1):
                    ag(unit, dr, step - 1, 1).wait_recv()
                    start(ag(unit, dr, step, 0))
        elif kind == 1:
            for dr in (1, -1):
                ag(unit, dr, 4, 1).wait_recv()
            start(ad(unit, c))
        else:
            ad(unit, 1 - c).wait_recv()
            ad(NG + unit, 1 - c).wait_recv()
            forward(unit)
        if n == 3:
            start(shift)
            xt[:, 0:L] = xv[0].T
        if n == 7:
            swap_x.wait_recv()
            xt[:, L : 2 * L] = xv[1].T

    loads[2].wait()
    shift.wait_recv()
    RB = 64

    @pl.loop(0, L // RB)
    def _(i):
        sl = pl.ds(pl.multiple_of(i * RB, RB), RB)
        mixed = mx[sl, :]
        row = lax.broadcasted_iota(jnp.int32, (RB, 1), 0) + i * RB
        live = jnp.where(row < length, 1.0, 0.0)
        cot = ct[sl, :].astype(F32) * live
        dn = cot * gt[sl, :].astype(F32)
        m1 = jnp.sum(dn, axis=-1, keepdims=True) * (1.0 / D)
        cen = mixed - jnp.sum(mixed, axis=-1, keepdims=True) * (1.0 / D)
        var = jnp.sum(cen * cen, axis=-1, keepdims=True) * (1.0 / D)
        m2 = jnp.sum(dn * cen, axis=-1, keepdims=True) * (1.0 / D)
        r = lax.rsqrt(var + 1e-05)
        ggb[sl, :] = (cot * (cen * r)).astype(BF16)
        dm[sl, :] = (r * (dn - m1 - cen * (m2 * r * r))).astype(BF16)

    outs = [pltpu.make_async_copy(ggb, gg_hbm, o_sem.at[0])]
    outs[0].start()

    def swap(g, half):
        return remote(gp.at[g, half], gx.at[g], ex_s.at[g], ex_r.at[g], sib)

    def backward(g):
        for hh in range(2):
            h = 2 * g + hh
            cq = slice(hh * DH, (hh + 1) * DH)
            ck = slice(256 + hh * DH, 256 + (hh + 1) * DH)
            ch = slice(h * DH, (h + 1) * DH)
            datt = dot(dm[:, ch], vv[:, ch], NT).astype(BF16).astype(F32)
            ds = (datt * dsc[h]).astype(BF16)
            dq = dot(ds, qk[g, :, ck]).astype(BF16).astype(F32)
            gp[g, 0, :, cq] = (dq * dact[g, :, cq]).astype(BF16)
            dk = dot(ds, qk[g, :, cq], TN).astype(BF16).astype(F32)
            gp[g, 1, :, cq] = (dk * dact[g, :, ck]).astype(BF16)
        start(swap(g, 1 - c))

    def term(g):
        swap(g, 1 - c).wait_recv()
        full = dot(xt[:, 0:L], gp[g, c]) + dot(xt[:, L : 2 * L], gx[g])
        tm[g] = full.reshape(Y, 2, 64, 256)

    def zz_of(unit):
        return 1 - zh if unit < NG else zh

    def rs(unit, dr, step):
        di = 0 if dr == 1 else 1
        src, dst = sb.at[unit, di, step - 1], rb.at[unit, di, step - 1]
        if step == 1:
            src, dst = src.at[pl.ds(0, 32)], dst.at[pl.ds(0, 32)]
        return remote(src, dst, rs_s.at[unit, di, step - 1], rs_r.at[unit, di, step - 1], nxt[dr])

    def rs_send(unit, dr, step):
        di = 0 if dr == 1 else 1
        own = tm.at[unit % NG, ring(y + dr * (5 - step)), zz_of(unit)]
        lo, hi = (0, 32) if dr == 1 else (32, 0)
        if step == 1:
            sb[unit, di, 0, 0:32] = own[lo : lo + 32].astype(BF16)
        elif step == 2:
            part = own[lo : lo + 32] + rb[unit, di, 0, 0:32].astype(F32)
            sb[unit, di, 1, lo : lo + 32] = part.astype(BF16)
            sb[unit, di, 1, hi : hi + 32] = own[hi : hi + 32].astype(BF16)
        else:
            sb[unit, di, step - 1] = (own[...] + rb[unit, di, step - 2].astype(F32)).astype(BF16)
        start(rs(unit, dr, step))

    def rz(g):
        return remote(zs.at[g], zr.at[g], rz_s.at[g], rz_r.at[g], opp)

    def col(g, cc):
        return pl.ds(pl.multiple_of(cc * D + g * 256, 256), 256)

    def rf(g, cc):
        return remote(fb.at[g, 1 - c], gwb.at[:, col(g, cc)], rf_s.at[g], rf_r.at[g], sib)

    def rs_end(unit):
        g = unit % NG
        for dr in (1, -1):
            rs(unit, dr, 4).wait_recv()
        full = tm[g, y, zz_of(unit)] + rb[unit, 0, 3].astype(F32) + rb[unit, 1, 3].astype(F32)
        if unit < NG:
            zs[g] = full.astype(BF16)
            start(rz(g))
        else:
            rz(g).wait_recv()
            full = full + zr[g].astype(F32)
            fb[g] = full.reshape(2, 32, 256)
            start(rf(g, c))
            gwb[:, col(g, c)] = fb[g, c]

    def grad_values(h):
        ch = slice(h * DH, (h + 1) * DH)
        gvb[:, ch] = dot(at[h], dm[:, ch], TN).astype(BF16)

    def grad_inputs(n):
        acc = jnp.zeros((L, 256), F32)
        for g in range(NG):
            for half in range(2):
                wg = wb[g, 2 * n : 2 * n + 2, :, :, :, half * 256 : (half + 1) * 256]
                acc = acc + dot(gp[g, half], wg.reshape(256, 256), NT)
        gib[:, n * 256 : (n + 1) * 256] = acc.astype(BF16)

    FILL = 17
    for n, token in enumerate(SCATTER):
        kind, unit = divmod(token, 100)
        if kind == 0:
            unit, step = divmod(unit, 10)
            for dr in (1, -1):
                if step > 1:
                    rs(unit, dr, step - 1).wait_recv()
                rs_send(unit, dr, step)
        elif kind == 1:
            backward(unit)
        elif kind == 2:
            term(unit)
        else:
            rs_end(unit)
        n -= FILL
        if 0 <= n < H:
            grad_values(n)
            if n == H - 1:
                outs.append(pltpu.make_async_copy(gvb, gv_hbm, o_sem.at[1]))
                outs[-1].start()
        elif H <= n < H + 4:
            grad_inputs(n - H)
            if n == H + 3:
                outs.append(pltpu.make_async_copy(gib, gi_hbm, o_sem.at[2]))
                outs[-1].start()
    for g in range(NG):
        rf(g, 1 - c).wait_recv()
    outs.append(pltpu.make_async_copy(gwb, gw_hbm, o_sem.at[3]))
    outs[-1].start()
    for cp in sent:
        cp.wait_send()
    for cp in outs:
        cp.wait()


def fused(x, v, g, og, lengths, w):
    any_space = pl.BlockSpec(memory_space=pl.ANY)
    dma = pltpu.SemaphoreType.DMA
    seq = (L, D)
    return pl.pallas_call(
        kernel,
        out_shape=(
            jax.ShapeDtypeStruct(seq, BF16),
            jax.ShapeDtypeStruct(seq, BF16),
            jax.ShapeDtypeStruct(seq, BF16),
            jax.ShapeDtypeStruct((32, 2 * D), F32),
        ),
        in_specs=[any_space] * 4 + [pl.BlockSpec(memory_space=pltpu.SMEM), any_space],
        out_specs=(any_space,) * 4,
        scratch_shapes=[
            pltpu.VMEM((NG, Y, 2, 2, 32, 512), BF16),
            pltpu.VMEM((2, L, D), BF16),
            pltpu.VMEM(seq, BF16),
            pltpu.VMEM(seq, BF16),
            pltpu.VMEM(seq, BF16),
            pltpu.VMEM((D, 2 * L), BF16),
            pltpu.VMEM((L, L), F32),
            pltpu.VMEM((NG, L, 512), F32),
            pltpu.VMEM((NG, L, 512), BF16),
            pltpu.VMEM((H, L, L), F32),
            pltpu.VMEM((H, L, L), BF16),
            pltpu.VMEM(seq, F32),
            pltpu.VMEM(seq, BF16),
            pltpu.VMEM((NG, 2, L, 256), BF16),
            pltpu.VMEM((NG, L, 256), BF16),
            pltpu.VMEM((NG, Y, 2, 64, 256), F32),
            pltpu.VMEM((2 * NG, 2, 4, 64, 256), BF16),
            pltpu.VMEM((2 * NG, 2, 4, 64, 256), BF16),
            pltpu.VMEM((NG, 64, 256), BF16),
            pltpu.VMEM((NG, 64, 256), BF16),
            pltpu.VMEM((NG, 2, 32, 256), F32),
            pltpu.VMEM((32, 2 * D), F32),
            pltpu.VMEM(seq, BF16),
            pltpu.VMEM(seq, BF16),
            pltpu.VMEM(seq, BF16),
            dma((11,)),
            dma((4,)),
            dma((2 * NG, 2, 4)),
            dma((2 * NG, 2, 4)),
            dma((NG,)),
            dma((NG,)),
            dma((2 * NG,)),
            dma((2 * NG,)),
            dma((2,)),
            dma((2,)),
            dma((NG,)),
            dma((NG,)),
            dma((2 * NG, 2, 4)),
            dma((2 * NG, 2, 4)),
            dma((NG,)),
            dma((NG,)),
            dma((NG,)),
            dma((NG,)),
        ],
        compiler_params=pltpu.CompilerParams(
            collective_id=0, has_side_effects=True, vmem_limit_bytes=60 * 1024 * 1024
        ),
        name="fused",
    )(x, v, g, og, lengths, w)


def hand_over(n, *refs):
    sources, targets, rooms, sems = refs[:n], refs[n : 2 * n], refs[2 * n : 3 * n], refs[3 * n]
    reads = [pltpu.make_async_copy(sources[i], rooms[i], sems.at[0, i]) for i in range(n)]
    writes = [pltpu.make_async_copy(rooms[i], targets[i], sems.at[1, i]) for i in range(n)]
    for cp in reads:
        cp.start()
    for i in range(n):
        reads[i].wait()
        writes[i].start()
    for cp in writes:
        cp.wait()


def finish(*arrays):
    n = len(arrays)
    any_space = pl.BlockSpec(memory_space=pl.ANY)
    return pl.pallas_call(
        functools.partial(hand_over, n),
        out_shape=tuple(jax.ShapeDtypeStruct(a.shape, a.dtype) for a in arrays),
        in_specs=[any_space] * n,
        out_specs=(any_space,) * n,
        scratch_shapes=[pltpu.VMEM(a.shape, a.dtype) for a in arrays]
        + [pltpu.SemaphoreType.DMA((2, n))],
        compiler_params=pltpu.CompilerParams(vmem_limit_bytes=60 * 1024 * 1024),
        name="finish",
    )(*arrays)


def on_device(inputs, values, gate_values, out_grad, lengths, qk_weight):
    gi, gv, gg, gw = fused(
        inputs[0, 0], values[0, 0], gate_values[0, 0], out_grad[0, 0], lengths, qk_weight[0]
    )
    gi, gv, gg, gw = finish(gi, gv, gg, gw)
    return (gi[None, None], gv[None, None], gg[None, None], gw[None])


def solution(mesh):
    seq = P("segment", "dp", None, None)
    return jax.shard_map(
        on_device,
        mesh=mesh,
        in_specs=(seq, seq, seq, seq, P("segment", "dp"), P("segment", "dp", None)),
        out_specs=(seq, seq, seq, P("segment", "dp", None)),
        check_vma=False,
    )
```

```python
import functools

import jax
import jax.numpy as jnp
from jax import lax
from jax.experimental import pallas as pl
from jax.experimental.pallas import tpu as pltpu
from jax.sharding import PartitionSpec as P

MESH = pl.DeviceIdType.MESH
H = 8
DH = 128
L = 256
D = 1024
SCALE = DH ** (-0.5)
Y = 8
Z_LO = 6
Z = 12
NG = 4
GATHER = (1, 21, 31, 11, 2, 22, 12, 32, 3, 23, 41, 13, 51, 61, 71, 24)
GATHER += (42, 33, 52, 62, 72, 4, 43, 102, 14, 53, 63, 73, 34, 44, 101, 100)
GATHER += (54, 64, 74, 104, 103, 105, 106, 200, 107, 201, 202, 203)
SCATTER = (102, 103, 100, 202, 101, 21, 203, 31, 61, 200, 1, 201, 11, 71, 22, 32)
SCATTER += (62, 2, 12, 41, 51, 23, 33, 72, 3, 13, 42, 24, 34, 52, 4, 14)
SCATTER += (63, 73, 43, 302, 303, 53, 300, 301, 64, 74, 44, 54, 306, 307, 304, 305)
F32 = jnp.float32
BF16 = jnp.bfloat16

NT = (((1,), (1,)), ((), ()))
TN = (((0,), (0,)), ((), ()))


def dot(a, b, dims=(((1,), (0,)), ((), ()))):
    return lax.dot_general(a, b, dims, preferred_element_type=F32)


def sigmoid(v):
    return 0.5 * jnp.tanh(0.5 * v) + 0.5


def kernel(
    x_hbm,
    v_hbm,
    g_hbm,
    og_hbm,
    len_hbm,
    w_hbm,
    gi_hbm,
    gv_hbm,
    gg_hbm,
    gw_hbm,
    wb,
    xv,
    vv,
    gt,
    ct,
    xt,
    mask,
    dact,
    qk,
    dsc,
    at,
    mx,
    dm,
    gp,
    gx,
    tm,
    sb,
    rb,
    zs,
    zr,
    fb,
    gwb,
    gib,
    ggb,
    gvb,
    len_ref,
    l_sem,
    o_sem,
    ag_s,
    ag_r,
    az_s,
    az_r,
    ad_s,
    ad_r,
    m_s,
    m_r,
    ex_s,
    ex_r,
    rs_s,
    rs_r,
    rz_s,
    rz_r,
    rf_s,
    rf_r,
):
    d = lax.axis_index("dp")
    seg = lax.axis_index("segment")
    nseg = lax.axis_size("segment")
    c = lax.rem(d, 2)
    zh = lax.rem(lax.div(d, 2), 2)
    y = lax.div(d, 4)

    def ring(i):
        return lax.rem(i + 2 * Y, Y)

    def dp_of(yy, zz, cc):
        return (yy * 2 + zz) * 2 + cc

    sib = {"dp": dp_of(y, zh, 1 - c)}
    opp = {"dp": dp_of(y, 1 - zh, c)}
    nxt = {1: {"dp": dp_of(ring(y + 1), zh, c)}, -1: {"dp": dp_of(ring(y - 1), zh, c)}}
    behind = {"segment": lax.rem(seg + nseg - 1, nseg)}
    ahead = {"segment": lax.rem(seg + 1, nseg)}

    barrier = pltpu.get_barrier_semaphore()
    for peer in (nxt[1], nxt[-1], sib, opp, behind, ahead):
        pl.semaphore_signal(barrier, inc=1, device_id=peer, device_id_type=MESH)

    def remote(src, dst, s, r, dev):
        return pltpu.make_async_remote_copy(
            src_ref=src, dst_ref=dst, send_sem=s, recv_sem=r, device_id=dev, device_id_type=MESH
        )

    stage = []
    for g in range(NG):
        for half in range(2):
            stage.append(
                pltpu.make_async_copy(
                    w_hbm.at[:, pl.ds(half * D + g * 256, 256)],
                    wb.at[g, y, zh, c, :, pl.ds(half * 256, 256)],
                    l_sem.at[2 * g + half],
                )
            )
    for cp in stage:
        cp.start()
    loads = [
        pltpu.make_async_copy(x_hbm, xv.at[0], l_sem.at[8]),
        pltpu.make_async_copy(v_hbm, vv, l_sem.at[9]),
        pltpu.make_async_copy(g_hbm, gt, l_sem.at[10]),
        pltpu.make_async_copy(len_hbm, len_ref, l_sem.at[11]),
    ]
    for cp in loads:
        cp.start()
    for cp in stage:
        cp.wait()
    pl.semaphore_wait(barrier, 6)

    sent = []

    def start(cp):
        cp.start()
        sent.append(cp)

    def ag_ref(g, yy, zz, dr, step):
        if step == 4:
            return wb.at[g, yy, zz, c, pl.ds(0 if dr == 1 else 16, 16)]
        return wb.at[g, yy, zz, c]

    def ag(unit, dr, step, back):
        part, g = divmod(unit, NG)
        zz = zh if part == 0 else 1 - zh
        ref = ag_ref(g, ring(y - dr * (step - 1 + back)), zz, dr, step)
        di = 0 if dr == 1 else 1
        return remote(ref, ref, ag_s.at[unit, di, step - 1], ag_r.at[unit, di, step - 1], nxt[dr])

    def az(g, zz):
        ref = wb.at[g, y, zz, c]
        return remote(ref, ref, az_s.at[g], az_r.at[g], opp)

    def ad(unit, cc):
        part, g = divmod(unit, NG)
        zz = zh if part == 0 else 1 - zh
        ref = wb.at[g, :, zz, cc]
        return remote(ref, ref, ad_s.at[unit], ad_r.at[unit], sib)

    def issue(unit):
        if unit >= NG:
            az(unit - NG, 1 - zh).wait_recv()
        for dr in (1, -1):
            start(ag(unit, dr, 1, 0))

    for g in range(NG):
        start(az(g, zh))
    for token in GATHER[:NG]:
        issue(token // 10)
    swap_x = remote(x_hbm, xv.at[1], m_s.at[0], m_r.at[0], sib)
    start(swap_x)
    shift = remote(og_hbm, ct, m_s.at[1], m_r.at[1], behind)

    rows = lax.broadcasted_iota(jnp.int32, (L, L), 0)
    cols = lax.broadcasted_iota(jnp.int32, (L, L), 1)
    loads[3].wait()
    length = len_ref[0, 0]
    mask[...] = jnp.where((cols <= rows) & (rows < length), 1.0, 0.0)
    loads[0].wait()
    loads[1].wait()

    def forward(g):
        wg = wb[g].reshape(D, 512)
        pre = dot(xv[0], wg)
        sg = sigmoid(pre)
        act = pre * sg
        dact[g] = sg + act - act * sg
        actb = act.astype(BF16)
        qk[g] = actb
        for hh in range(2):
            h = 2 * g + hh
            q = actb[:, hh * DH : (hh + 1) * DH]
            k = actb[:, 256 + hh * DH : 256 + (hh + 1) * DH]
            s = dot(q, k, NT) * SCALE
            ss = sigmoid(s)
            sa = s * ss
            m = mask[...]
            att = (sa * m).astype(BF16)
            at[h] = att
            dsc[h] = (ss + sa - sa * ss) * (m * SCALE)
            mx[:, h * DH : (h + 1) * DH] = dot(att, vv[:, h * DH : (h + 1) * DH])

    for n, token in enumerate(GATHER[4:]):
        kind, unit = divmod(token, 100)
        if kind == 0:
            unit, step = divmod(unit, 10)
            if step == 1:
                issue(unit)
            else:
                for dr in (1, -1):
                    ag(unit, dr, step - 1, 1).wait_recv()
                    start(ag(unit, dr, step, 0))
        elif kind == 1:
            for dr in (1, -1):
                ag(unit, dr, 4, 1).wait_recv()
            start(ad(unit, c))
        else:
            ad(unit, 1 - c).wait_recv()
            ad(NG + unit, 1 - c).wait_recv()
            forward(unit)
        if n == 3:
            start(shift)
            xt[:, 0:L] = xv[0].T
        if n == 7:
            swap_x.wait_recv()
            xt[:, L : 2 * L] = xv[1].T

    loads[2].wait()
    shift.wait_recv()
    RB = 64

    @pl.loop(0, L // RB)
    def _(i):
        sl = pl.ds(pl.multiple_of(i * RB, RB), RB)
        mixed = mx[sl, :]
        row = lax.broadcasted_iota(jnp.int32, (RB, 1), 0) + i * RB
        live = jnp.where(row < length, 1.0, 0.0)
        cot = ct[sl, :].astype(F32) * live
        dn = cot * gt[sl, :].astype(F32)
        m1 = jnp.sum(dn, axis=-1, keepdims=True) * (1.0 / D)
        cen = mixed - jnp.sum(mixed, axis=-1, keepdims=True) * (1.0 / D)
        var = jnp.sum(cen * cen, axis=-1, keepdims=True) * (1.0 / D)
        m2 = jnp.sum(dn * cen, axis=-1, keepdims=True) * (1.0 / D)
        r = lax.rsqrt(var + 1e-05)
        ggb[sl, :] = (cot * (cen * r)).astype(BF16)
        dm[sl, :] = (r * (dn - m1 - cen * (m2 * r * r))).astype(BF16)

    outs = [pltpu.make_async_copy(ggb, gg_hbm, o_sem.at[0])]
    outs[0].start()

    def swap(g, half):
        return remote(gp.at[g, half], gx.at[g], ex_s.at[g], ex_r.at[g], sib)

    def backward(g):
        for hh in range(2):
            h = 2 * g + hh
            cq = slice(hh * DH, (hh + 1) * DH)
            ck = slice(256 + hh * DH, 256 + (hh + 1) * DH)
            ch = slice(h * DH, (h + 1) * DH)
            datt = dot(dm[:, ch], vv[:, ch], NT).astype(BF16).astype(F32)
            ds = (datt * dsc[h]).astype(BF16)
            dq = dot(ds, qk[g, :, ck]).astype(BF16).astype(F32)
            gp[g, 0, :, cq] = (dq * dact[g, :, cq]).astype(BF16)
            dk = dot(ds, qk[g, :, cq], TN).astype(BF16).astype(F32)
            gp[g, 1, :, cq] = (dk * dact[g, :, ck]).astype(BF16)
        start(swap(g, 1 - c))

    def term(g):
        swap(g, 1 - c).wait_recv()
        full = dot(xt[:, 0:L], gp[g, c]) + dot(xt[:, L : 2 * L], gx[g])
        tm[g] = full.reshape(Y, 2, 64, 256)

    def zz_of(unit):
        return 1 - zh if unit < NG else zh

    def rs(unit, dr, step):
        di = 0 if dr == 1 else 1
        src, dst = sb.at[unit, di, step - 1], rb.at[unit, di, step - 1]
        if step == 1:
            src, dst = src.at[pl.ds(0, 32)], dst.at[pl.ds(0, 32)]
        return remote(src, dst, rs_s.at[unit, di, step - 1], rs_r.at[unit, di, step - 1], nxt[dr])

    def rs_send(unit, dr, step):
        di = 0 if dr == 1 else 1
        own = tm.at[unit % NG, ring(y + dr * (5 - step)), zz_of(unit)]
        lo, hi = (0, 32) if dr == 1 else (32, 0)
        if step == 1:
            sb[unit, di, 0, 0:32] = own[lo : lo + 32].astype(BF16)
        elif step == 2:
            part = own[lo : lo + 32] + rb[unit, di, 0, 0:32].astype(F32)
            sb[unit, di, 1, lo : lo + 32] = part.astype(BF16)
            sb[unit, di, 1, hi : hi + 32] = own[hi : hi + 32].astype(BF16)
        else:
            sb[unit, di, step - 1] = (own[...] + rb[unit, di, step - 2].astype(F32)).astype(BF16)
        start(rs(unit, dr, step))

    def rz(g):
        return remote(zs.at[g], zr.at[g], rz_s.at[g], rz_r.at[g], opp)

    def col(g, cc):
        return pl.ds(pl.multiple_of(cc * D + g * 256, 256), 256)

    def rf(g, cc):
        return remote(fb.at[g, 1 - c], gwb.at[:, col(g, cc)], rf_s.at[g], rf_r.at[g], sib)

    def rs_end(unit):
        g = unit % NG
        for dr in (1, -1):
            rs(unit, dr, 4).wait_recv()
        full = tm[g, y, zz_of(unit)] + rb[unit, 0, 3].astype(F32) + rb[unit, 1, 3].astype(F32)
        if unit < NG:
            zs[g] = full.astype(BF16)
            start(rz(g))
        else:
            rz(g).wait_recv()
            full = full + zr[g].astype(F32)
            fb[g] = full.reshape(2, 32, 256)
            start(rf(g, c))
            gwb[:, col(g, c)] = fb[g, c]

    def grad_values(h):
        ch = slice(h * DH, (h + 1) * DH)
        gvb[:, ch] = dot(at[h], dm[:, ch], TN).astype(BF16)

    def grad_inputs(n):
        acc = jnp.zeros((L, 256), F32)
        for g in range(NG):
            for half in range(2):
                wg = wb[g, 2 * n : 2 * n + 2, :, :, :, half * 256 : (half + 1) * 256]
                acc = acc + dot(gp[g, half], wg.reshape(256, 256), NT)
        gib[:, n * 256 : (n + 1) * 256] = acc.astype(BF16)

    def drain(keep):
        while len(sent) > keep:
            sent.pop(0).wait_send()

    gathered = len(sent)
    FILL = 17
    for n, token in enumerate(SCATTER):
        kind, unit = divmod(token, 100)
        if kind == 0:
            unit, step = divmod(unit, 10)
            for dr in (1, -1):
                if step > 1:
                    rs(unit, dr, step - 1).wait_recv()
                rs_send(unit, dr, step)
        elif kind == 1:
            backward(unit)
        elif kind == 2:
            term(unit)
        else:
            rs_end(unit)
        if n == FILL - 1:
            drain(len(sent) - gathered)
        if n == len(SCATTER) - 6:
            drain(28)
        n -= FILL
        if 0 <= n < H:
            grad_values(n)
            if n == H - 1:
                outs.append(pltpu.make_async_copy(gvb, gv_hbm, o_sem.at[1]))
                outs[-1].start()
        elif H <= n < H + 4:
            grad_inputs(n - H)
            if n == H + 3:
                outs.append(pltpu.make_async_copy(gib, gi_hbm, o_sem.at[2]))
                outs[-1].start()
    for g in range(NG):
        rf(g, 1 - c).wait_recv()
    outs.append(pltpu.make_async_copy(gwb, gw_hbm, o_sem.at[3]))
    outs[-1].start()
    for cp in sent:
        cp.wait_send()
    for cp in outs:
        cp.wait()


def fused(x, v, g, og, lengths, w):
    any_space = pl.BlockSpec(memory_space=pl.ANY)
    dma = pltpu.SemaphoreType.DMA
    seq = (L, D)
    return pl.pallas_call(
        kernel,
        out_shape=(
            jax.ShapeDtypeStruct(seq, BF16),
            jax.ShapeDtypeStruct(seq, BF16),
            jax.ShapeDtypeStruct(seq, BF16),
            jax.ShapeDtypeStruct((32, 2 * D), F32),
        ),
        in_specs=[any_space] * 6,
        out_specs=(any_space,) * 4,
        scratch_shapes=[
            pltpu.VMEM((NG, Y, 2, 2, 32, 512), BF16),
            pltpu.VMEM((2, L, D), BF16),
            pltpu.VMEM(seq, BF16),
            pltpu.VMEM(seq, BF16),
            pltpu.VMEM(seq, BF16),
            pltpu.VMEM((D, 2 * L), BF16),
            pltpu.VMEM((L, L), F32),
            pltpu.VMEM((NG, L, 512), F32),
            pltpu.VMEM((NG, L, 512), BF16),
            pltpu.VMEM((H, L, L), F32),
            pltpu.VMEM((H, L, L), BF16),
            pltpu.VMEM(seq, F32),
            pltpu.VMEM(seq, BF16),
            pltpu.VMEM((NG, 2, L, 256), BF16),
            pltpu.VMEM((NG, L, 256), BF16),
            pltpu.VMEM((NG, Y, 2, 64, 256), F32),
            pltpu.VMEM((2 * NG, 2, 4, 64, 256), BF16),
            pltpu.VMEM((2 * NG, 2, 4, 64, 256), BF16),
            pltpu.VMEM((NG, 64, 256), BF16),
            pltpu.VMEM((NG, 64, 256), BF16),
            pltpu.VMEM((NG, 2, 32, 256), F32),
            pltpu.VMEM((32, 2 * D), F32),
            pltpu.VMEM(seq, BF16),
            pltpu.VMEM(seq, BF16),
            pltpu.VMEM(seq, BF16),
            pltpu.SMEM((1, 1), jnp.int32),
            dma((12,)),
            dma((4,)),
            dma((2 * NG, 2, 4)),
            dma((2 * NG, 2, 4)),
            dma((NG,)),
            dma((NG,)),
            dma((2 * NG,)),
            dma((2 * NG,)),
            dma((2,)),
            dma((2,)),
            dma((NG,)),
            dma((NG,)),
            dma((2 * NG, 2, 4)),
            dma((2 * NG, 2, 4)),
            dma((NG,)),
            dma((NG,)),
            dma((NG,)),
            dma((NG,)),
        ],
        compiler_params=pltpu.CompilerParams(
            collective_id=0, has_side_effects=True, vmem_limit_bytes=60 * 1024 * 1024
        ),
        name="fused",
    )(x, v, g, og, lengths, w)


def hand_over(n, *refs):
    sources, targets, rooms, sems = refs[:n], refs[n : 2 * n], refs[2 * n : 3 * n], refs[3 * n]
    reads = [pltpu.make_async_copy(sources[i], rooms[i], sems.at[0, i]) for i in range(n)]
    writes = [pltpu.make_async_copy(rooms[i], targets[i], sems.at[1, i]) for i in range(n)]
    for cp in reads:
        cp.start()
    for i in range(n):
        reads[i].wait()
        writes[i].start()
    for cp in writes:
        cp.wait()


def finish(*arrays):
    n = len(arrays)
    any_space = pl.BlockSpec(memory_space=pl.ANY)
    return pl.pallas_call(
        functools.partial(hand_over, n),
        out_shape=tuple(jax.ShapeDtypeStruct(a.shape, a.dtype) for a in arrays),
        in_specs=[any_space] * n,
        out_specs=(any_space,) * n,
        scratch_shapes=[pltpu.VMEM(a.shape, a.dtype) for a in arrays]
        + [pltpu.SemaphoreType.DMA((2, n))],
        compiler_params=pltpu.CompilerParams(vmem_limit_bytes=60 * 1024 * 1024),
        name="finish",
    )(*arrays)


def on_device(inputs, values, gate_values, out_grad, lengths, qk_weight):
    gi, gv, gg, gw = fused(
        inputs[0, 0], values[0, 0], gate_values[0, 0], out_grad[0, 0], lengths, qk_weight[0]
    )
    gi, gv, gg, gw = finish(gi, gv, gg, gw)
    return (gi[None, None], gv[None, None], gg[None, None], gw[None])


def solution(mesh):
    seq = P("segment", "dp", None, None)
    return jax.shard_map(
        on_device,
        mesh=mesh,
        in_specs=(seq, seq, seq, seq, P("segment", "dp"), P("segment", "dp", None)),
        out_specs=(seq, seq, seq, P("segment", "dp", None)),
        check_vma=False,
    )
```
